768 devices in a mesh: dp: 48 (over z_lo, y), fsdp: 16 (over x, z_hi, core).
Axes of the slice: x: 4, y: 8, z: 12 (z_hi: 2, z_lo: 6; z = z_hi * 6 + z_lo), core: 2. Of those that a mesh axis runs over, the one named last changes fastest.
Arguments:
- hidden_in: bfloat16 [98304, 14336], P(('dp', 'fsdp')), may hold values from -6 to 6
- out_grads: bfloat16 [98304, 4096], P(('dp', 'fsdp')), may hold values from -6 to 6
- piece_of: int32 [768, 128], P(('dp', 'fsdp')), may hold values from 0 to 47, never falling along the last dimension, each value on 1 to 5 neighbouring positions
- owner_dp: int32 [768, 48], P(('dp', 'fsdp')), may hold values from 0 to 47, as said below
- owner_slot: int32 [768, 48], P(('dp', 'fsdp')), may hold values from 0 to 23
- sketch_in: bfloat16 [14336, 64], P('fsdp'), may hold values from -0.046875 to 0.046875
- sketch_out: bfloat16 [4096, 64], P('fsdp'), may hold values from -0.09375 to 0.09375
Outputs:
- gram: float32 [192, 4096], P('dp', 'fsdp')
The draws below stay inside these ranges and needn't reach their ends.
Inputs may be any that keep to these rules, and one draw needn't show every extreme that they name: `owner_dp`: each device sends exactly 2 pieces to each of 24 cyclically consecutive dp indices and none to the others; the first of these dp indices is the sender's dp index plus an offset that is the same for all devices that share an fsdp index, modulo 48.
All inputs are finite; a program needn't handle non-finite values.
Results may differ from the reference program's by a relative error of at most 0.0036.
Values may be sent and summed in bfloat16 or wider, within the bound.
A program may use at most 32 MiB of HBM per device.

```python
import math
import jax
import jax.numpy as jnp
import numpy as np
from jax import lax

D = 4096
FF = 14336
R = 64
CAP = 2
GR = 192
TOK_DEV = 128
PIECES = 48
EX_OWN = 24
EXAMPLES = 18432
TOKENS = 98304
N_DP = 48
N_FSDP = 16
DEVICES = 768


def draw_owner_dp(key, part):
    rotate_key, order_key = jax.random.split(jax.random.fold_in(key, 17))
    rotation = jax.random.randint(rotate_key, (N_FSDP,), 0, N_DP).astype(jnp.int32)
    scores = jax.random.randint(order_key, (DEVICES, PIECES), 0, 1 << 20).astype(jnp.int32) * PIECES
    scores = scores + jnp.arange(PIECES, dtype=jnp.int32)[None, :]
    ranking = jnp.argsort(scores, axis=1, stable=True).astype(jnp.int32)
    device_ids = jnp.arange(DEVICES, dtype=jnp.int32)
    column = device_ids % N_FSDP
    group_row = device_ids // N_FSDP
    start_index = (rotation[column] + group_row).astype(jnp.int32)
    shifted = ranking // CAP + start_index[:, None]
    return (shifted % N_DP).astype(jnp.int32)


def set_ends(result, own_key, smallest, high):
    index_at = [jax.random.randint(jax.random.fold_in(own_key, axis), (), 0, length) for axis, length in enumerate(result.shape)]
    widest = result.shape.index(max(result.shape))
    neighbour = index_at[:widest] + [(index_at[widest] + 1) % result.shape[widest]] + index_at[widest + 1:]
    return result.at[tuple(index_at)].set(smallest).at[tuple(neighbour)].set(high)


def shard_levels(rng, shape, pieces, smallest, largest):
    loudness, own = 1.0, jax.random.fold_in(rng, 6)
    for axis_at, shards_of in pieces:
        draws = jnp.exp(jax.random.uniform(jax.random.fold_in(own, axis_at), (shards_of,), jnp.float32, smallest / len(pieces), largest / len(pieces)))
        loudness = loudness * jnp.repeat(draws, shape[axis_at] // shards_of).reshape([-1 if axis == axis_at else 1 for axis in range(len(shape))])
    return loudness


def length_profile(number_of, total, most, skew):
    weights = [(1 << 20) // math.isqrt(rank ** skew) + 1 for rank in range(2, number_of + 1)]
    spare, given = total - most - (number_of - 1), [1] * (number_of - 1)
    while spare > 0:
        movable = [i for i in range(number_of - 1) if given[i] < most]
        whole, left = sum([weights[i] for i in movable]), spare
        for i in movable:
            extra = min(most - given[i], max(1, left * weights[i] // whole), spare)
            given[i] = given[i] + extra
            spare = spare - extra
    return np.array([most] + given)


def ragged_sizes(key, count, total, bound, lean):
    if count == 2:
        one = jax.random.randint(key, (), max(1, total - bound), min(bound, total - 1) + 1)
        return jnp.stack([one, total - one])
    lengths = jnp.asarray(length_profile(count, total, bound, lean), jnp.int32)
    pairs = (count - 1) // 2
    giver, sink = lengths[1:1 + 2 * pairs:2], lengths[2:2 + 2 * pairs:2]
    room = jnp.minimum(giver - 1, bound - sink)
    moved = jax.random.randint(jax.random.fold_in(key, 1), (pairs,), 0, 1 << 20) % (room + 1)
    lengths = lengths.at[1:1 + 2 * pairs:2].set(giver - moved).at[2:2 + 2 * pairs:2].set(sink + moved)
    return lengths[jax.random.permutation(jax.random.fold_in(key, 2), count)]


def noise(key, dims, scale, most, shards=(), held_as=jnp.bfloat16):
    entries = jax.random.normal(key, dims, jnp.float32) * scale
    if len(shards) > 0:
        entries = shard_levels(key, dims, shards, -0.22, 0.18) * entries
    return jnp.clip(entries, min=-most, max=most).astype(held_as)


def setup_inputs(seed: int = 0) -> dict:
    seeds = jax.random.split(jax.random.key(seed), 8)
    hidden_in = noise(seeds[0], (TOKENS, FF), 1.0, 6.0, ((0, 768),))
    out_grads = noise(seeds[1], (TOKENS, D), 1.0, 6.0, ((0, 768),))
    piece_of = jax.vmap(lambda own: jnp.searchsorted(jnp.cumsum(ragged_sizes(own, PIECES, TOK_DEV, 2 * TOK_DEV // PIECES, 1)), jnp.arange(TOK_DEV), side="right"))(jax.random.split(seeds[2], DEVICES)).reshape((DEVICES, TOK_DEV)).astype(jnp.int32)
    owner_dp = draw_owner_dp(jax.random.fold_in(seeds[7], 71), 0)
    owner_slot = set_ends(jax.random.randint(seeds[4], (DEVICES, PIECES), 0, EX_OWN), jax.random.fold_in(seeds[4], 1), 0, EX_OWN - 1).astype(jnp.int32)
    sketch_in = noise(seeds[5], (FF, R), FF ** -0.5, 0.046875, ((0, 16),))
    sketch_out = noise(seeds[6], (D, R), D ** -0.5, 0.09375, ((0, 16),))
    return {"hidden_in": hidden_in, "out_grads": out_grads, "piece_of": piece_of, "owner_dp": owner_dp, "owner_slot": owner_slot, "sketch_in": sketch_in, "sketch_out": sketch_out}


def reference(hidden_in, out_grads, piece_of, owner_dp, owner_slot, sketch_in, sketch_out):
    device_count = N_DP * N_FSDP
    hidden_blocks = hidden_in.reshape(device_count, TOK_DEV, FF)
    grad_blocks = out_grads.reshape(device_count, TOK_DEV, D)

    def project(pack):
        hidden_rows, grad_rows, pieces_row = pack
        inputs_low = jnp.dot(hidden_rows, sketch_in, preferred_element_type=jnp.float32).astype(jnp.bfloat16)
        errors_low = jnp.dot(grad_rows, sketch_out, preferred_element_type=jnp.float32).astype(jnp.bfloat16)
        member = (pieces_row[:, None] == jnp.arange(PIECES, dtype=jnp.int32)[None, :]).astype(jnp.float32)
        outer = jnp.einsum('tp,ti,tj->pij', member, inputs_low.astype(jnp.float32), errors_low.astype(jnp.float32))
        return outer.reshape(PIECES, R * R)
    piece_features = lax.map(project, (hidden_blocks, grad_blocks, piece_of))
    column = (jnp.arange(device_count, dtype=jnp.int32) % N_FSDP).astype(jnp.int32)
    example_key = ((owner_dp * N_FSDP + column[:, None]) * EX_OWN + owner_slot).astype(jnp.int32)
    features = jax.ops.segment_sum(piece_features.reshape(device_count * PIECES, R * R), example_key.reshape(-1), num_segments=EXAMPLES)
    features = features.astype(jnp.bfloat16)
    gram = jnp.dot(features[:, :GR].T, features, preferred_element_type=jnp.float32)
    return gram * (1.0 / math.sqrt(EXAMPLES))
```

```python
import math

import jax
import jax.numpy as jnp
from jax import lax
from jax.sharding import PartitionSpec as P

CAP = 2
GR = 192
SPAN = 5
ROWS = 16


def pack_rows(factors, piece_of, target, slot):
    tokens = factors.shape[0]
    pieces = target.shape[0]
    count_dp = lax.axis_size("dp")
    number = jnp.arange(pieces, dtype=jnp.int32)
    member = piece_of[:, None] == number[None, :]
    first = jnp.sum((piece_of[:, None] < number[None, :]).astype(jnp.int32), axis=0)
    earlier = number[None, :] < number[:, None]
    ranked = jnp.sum(((target[:, None] == target[None, :]) & earlier).astype(jnp.int32), axis=1)
    base = target * ROWS + ranked * SPAN - first
    place = jnp.arange(tokens, dtype=jnp.int32) + jnp.sum(jnp.where(member, base[None, :], 0), axis=1)
    label_place = target * ROWS + CAP * SPAN + ranked
    every = jnp.arange(count_dp * ROWS, dtype=jnp.int32)[:, None]
    select = jnp.concatenate([every == place[None, :], every == label_place[None, :]], axis=1).astype(jnp.bfloat16)
    label_rows = jnp.broadcast_to((slot + 1).astype(jnp.bfloat16)[:, None], (pieces, factors.shape[1]))
    values = jnp.concatenate([factors, label_rows], axis=0)
    packed = jnp.dot(select, values, preferred_element_type=jnp.float32).astype(jnp.bfloat16)
    return packed.reshape(count_dp, ROWS, factors.shape[1])


def on_device(hidden_in, out_grads, piece_of, owner_dp, owner_slot, sketch_in, sketch_out):
    count_dp = lax.axis_size("dp")
    count_fsdp = lax.axis_size("fsdp")
    width = sketch_in.shape[1]
    owned = count_dp // 2
    full_in = lax.all_gather(sketch_in, "fsdp", axis=0, tiled=True)
    full_out = lax.all_gather(sketch_out, "fsdp", axis=0, tiled=True)
    inputs_low = jnp.dot(hidden_in, full_in, preferred_element_type=jnp.float32).astype(jnp.bfloat16)
    errors_low = jnp.dot(out_grads, full_out, preferred_element_type=jnp.float32).astype(jnp.bfloat16)
    factors = jnp.concatenate([inputs_low, errors_low], axis=1)
    packed = pack_rows(factors, piece_of[0], owner_dp[0], owner_slot[0])
    got = lax.all_to_all(packed, "dp", split_axis=0, concat_axis=0, tiled=True)
    labels = got[:, CAP * SPAN : CAP * SPAN + CAP, 0].astype(jnp.int32)
    labels = jnp.repeat(labels, SPAN, axis=1)
    rows = got[:, : CAP * SPAN].reshape(count_dp * CAP * SPAN, 2 * width)
    hit = (labels.reshape(-1)[:, None] == 1 + jnp.arange(owned, dtype=jnp.int32)[None, :]).astype(jnp.bfloat16)
    spread = rows[:, :width][:, :, None] * hit[:, None, :]
    spread = spread.reshape(rows.shape[0], width * owned)
    features = lax.dot_general(spread, rows[:, width:], (((0,), (0,)), ((), ())), preferred_element_type=jnp.float32)
    features = features.astype(jnp.bfloat16)
    share = width // count_fsdp
    head = GR // width
    blocks = features.reshape(count_fsdp, share * owned, width)
    first = jnp.broadcast_to(features[: head * owned][None], (count_fsdp, head * owned, width))
    outgoing = jnp.concatenate([blocks, first], axis=1)
    mixed = lax.all_to_all(outgoing, "fsdp", split_axis=0, concat_axis=0, tiled=True)
    mixed = mixed.reshape(count_fsdp, share + head, owned, width)
    right = mixed[:, :share].transpose(0, 2, 1, 3).reshape(count_fsdp * owned, share * width)
    left = mixed[:, share:].transpose(0, 2, 1, 3).reshape(count_fsdp * owned, head * width)
    local_gram = lax.dot_general(left, right, (((0,), (0,)), ((), ())), preferred_element_type=jnp.float32)
    terms = lax.all_to_all(
        local_gram.reshape(count_dp, GR // count_dp, share * width), "dp", split_axis=0, concat_axis=0, tiled=True
    )
    scale_factor = 1.0 / math.sqrt(owned * count_dp * count_fsdp)
    return jnp.sum(terms, axis=0) * scale_factor


def solution(mesh):
    return jax.shard_map(
        on_device,
        mesh=mesh,
        in_specs=(
            P(("dp", "fsdp"), None),
            P(("dp", "fsdp"), None),
            P(("dp", "fsdp"), None),
            P(("dp", "fsdp"), None),
            P(("dp", "fsdp"), None),
            P("fsdp", None),
            P("fsdp", None),
        ),
        out_specs=P("dp", "fsdp"),
        check_vma=False,
    )
```

```python
import math

import jax
import jax.numpy as jnp
from jax import lax
from jax.experimental import pallas as pl
from jax.experimental.pallas import tpu as pltpu
from jax.sharding import PartitionSpec as P

CAP = 2
GR = 192
SPAN = 5
ROWS = 16
NX, NY, NZ = 4, 8, 6
PARTS = 4
MESH = pl.DeviceIdType.MESH


def project_kernel(
    hidden_hbm, grads_hbm, in_hbm, out_hbm, low_ref,
    hidden, grads, held, acc_in, acc_out, load_sem, recv_sem, send_sem, edge_sem, inner_sem,
):
    d, f = lax.axis_index("dp"), lax.axis_index("fsdp")
    p, y = d // NY, d % NY
    x, h, c = f // 4, (f // 2) % 2, f % 2
    wide_in, wide_out = in_hbm.shape[1], out_hbm.shape[1]
    step_rows = held.shape[1] // PARTS

    def name(x_, h_, c_):
        return x_ * 4 + h_ * 2 + c_

    east, west, far = (x + 1) % NX, (x + 3) % NX, (x + 2) % NX
    up_p, down_p = (p + 1) % NZ, (p + NZ - 1) % NZ
    up_h, down_h = (h + (p + 1) // NZ) % 2, (h + 1 - (p + NZ - 1) // NZ) % 2
    to_east, to_west, to_twin = (d, name(east, h, c)), (d, name(west, h, c)), (d, name(x, h, 1 - c))
    to_up = (up_p * NY + y, name(x, up_h, c))
    to_down = (down_p * NY + y, name(x, down_h, c))
    half = p // 3
    depth = p + half * (5 - 2 * p)
    to_inner = tuple((1 - half) * a + half * b for a, b in zip(to_up, to_down))
    to_outer = tuple((1 - half) * b + half * a for a, b in zip(to_up, to_down))

    barrier = pltpu.get_barrier_semaphore()
    for peer in (to_east, to_west, to_twin, to_up, to_down):
        pl.semaphore_signal(barrier, inc=1, device_id=peer, device_id_type=MESH)

    loads = (
        pltpu.make_async_copy(in_hbm, held.at[f, :, pl.ds(0, wide_in)], load_sem.at[0]),
        pltpu.make_async_copy(out_hbm, held.at[f, :, pl.ds(wide_in, wide_out)], load_sem.at[1]),
        pltpu.make_async_copy(grads_hbm, grads, load_sem.at[2]),
        pltpu.make_async_copy(hidden_hbm, hidden, load_sem.at[3]),
    )
    for load in loads:
        load.start()

    def move(shard, part, peer, sem):
        piece = held.at[shard, pl.ds(pl.multiple_of(part * step_rows, step_rows), step_rows), :]
        return pltpu.make_async_remote_copy(
            src_ref=piece, dst_ref=piece, send_sem=sem, recv_sem=recv_sem.at[shard, part],
            device_id=peer, device_id_type=MESH,
        )

    def send(shard, part, *peers):
        for peer in peers:
            move(shard, part, peer, send_sem).start()

    def arrived(shard, part):
        move(shard, part, to_twin, send_sem).wait_recv()

    pl.semaphore_wait(barrier, 5)
    loads[0].wait()
    loads[1].wait()

    for part in range(PARTS):

        @pl.when(depth == 0)
        def _():
            move(f, part, to_outer, edge_sem).start()

        send(f, part, to_east, to_west, to_twin)

    def pass_on(h_, part):
        for from_x, ahead, goes in ((west, to_east, part < PARTS // 2), (east, to_west, part >= PARTS // 2)):
            shard = name(from_x, h_, c)
            arrived(shard, part)
            if isinstance(goes, bool):
                if goes:
                    send(shard, part, ahead)
            else:
                pl.when(goes)(lambda: send(shard, part, ahead))
            send(shard, part, to_twin)

    across = name(x, 1 - h, c)

    @pl.loop(0, 2 * PARTS)
    def _(t):
        @pl.when(t < PARTS)
        def _():
            pass_on(h, t)

        part = t - 2 * depth

        @pl.when(jnp.logical_and(part >= 0, part < PARTS))
        def _():
            arrived(across, part)

            @pl.when(depth < 2)
            def _():
                move(across, part, to_inner, inner_sem).start()

            send(across, part, to_east, to_west, to_twin)

    acc_in[...] = jnp.zeros_like(acc_in)
    acc_out[...] = jnp.zeros_like(acc_out)
    nt = (((1,), (1,)), ((), ()))

    def use(shard):
        a = hidden[:, pl.ds(pl.multiple_of(shard * wide_in, 128), wide_in)]
        acc_in[...] += lax.dot_general(a, held[shard, :, :wide_in], nt, preferred_element_type=jnp.float32)
        b = grads[:, pl.ds(pl.multiple_of(shard * wide_out, 128), wide_out)]
        acc_out[...] += lax.dot_general(b, held[shard, :, wide_in:], nt, preferred_element_type=jnp.float32)

    def take(shard):
        for part in range(PARTS):
            arrived(shard, part)
        use(shard)

    def relay_far(h_):
        for part in range(PARTS):
            arrived(name(far, h_, c), part)
            send(name(far, h_, c), part, to_twin)

    relay_far(h)
    for part in range(PARTS):
        pass_on(1 - h, part)
    loads[2].wait()
    loads[3].wait()
    for x_ in (x, west, east, far):
        use(name(x_, h, c))
    for x_ in (x, west, east):
        use(name(x_, 1 - h, c))
    relay_far(1 - h)
    use(name(far, 1 - h, c))
    for h_ in (h, 1 - h):
        for x_ in (x, west, east, far):
            take(name(x_, h_, 1 - c))

    low_ref[:, :64] = acc_in[...].astype(low_ref.dtype)
    low_ref[:, 64:] = acc_out[...].astype(low_ref.dtype)

    def drain(count, sem):
        whole = held.at[pl.ds(0, count)]
        pltpu.make_async_copy(whole, whole, sem).wait()

    drain(14, send_sem)

    @pl.when(depth == 0)
    def _():
        drain(1, edge_sem)

    @pl.when(depth < 2)
    def _():
        drain(1, inner_sem)


def project(hidden_in, out_grads, sketch_in, sketch_out):
    rows = hidden_in.shape[0]
    count = lax.axis_size("fsdp")
    width = sketch_in.shape[1]
    wide = sketch_in.shape[0] + sketch_out.shape[0]
    anywhere = pl.BlockSpec(memory_space=pl.ANY)
    return pl.pallas_call(
        project_kernel,
        out_shape=jax.ShapeDtypeStruct((rows, 2 * width), jnp.bfloat16),
        in_specs=[anywhere] * 4,
        out_specs=pl.BlockSpec(memory_space=pltpu.VMEM),
        scratch_shapes=[
            pltpu.VMEM(hidden_in.shape, jnp.bfloat16),
            pltpu.VMEM(out_grads.shape, jnp.bfloat16),
            pltpu.VMEM((count, width, wide), jnp.bfloat16),
            pltpu.VMEM((rows, width), jnp.float32),
            pltpu.VMEM((rows, width), jnp.float32),
            pltpu.SemaphoreType.DMA((4,)),
            pltpu.SemaphoreType.DMA((count, PARTS)),
            pltpu.SemaphoreType.DMA,
            pltpu.SemaphoreType.DMA,
            pltpu.SemaphoreType.DMA,
        ],
        compiler_params=pltpu.CompilerParams(collective_id=0, has_side_effects=True),
        name="project",
    )(hidden_in, out_grads, sketch_in.T, sketch_out.T)


def pack_rows(factors, piece_of, target, slot):
    tokens = factors.shape[0]
    pieces = target.shape[0]
    count_dp = lax.axis_size("dp")
    number = jnp.arange(pieces, dtype=jnp.int32)
    member = piece_of[:, None] == number[None, :]
    first = jnp.sum((piece_of[:, None] < number[None, :]).astype(jnp.int32), axis=0)
    earlier = number[None, :] < number[:, None]
    ranked = jnp.sum(((target[:, None] == target[None, :]) & earlier).astype(jnp.int32), axis=1)
    base = target * ROWS + ranked * SPAN - first
    place = jnp.arange(tokens, dtype=jnp.int32) + jnp.sum(jnp.where(member, base[None, :], 0), axis=1)
    label_place = target * ROWS + CAP * SPAN + ranked
    every = jnp.arange(count_dp * ROWS, dtype=jnp.int32)[:, None]
    select = jnp.concatenate([every == place[None, :], every == label_place[None, :]], axis=1).astype(jnp.bfloat16)
    label_rows = jnp.broadcast_to((slot + 1).astype(jnp.bfloat16)[:, None], (pieces, factors.shape[1]))
    values = jnp.concatenate([factors, label_rows], axis=0)
    packed = jnp.dot(select, values, preferred_element_type=jnp.float32).astype(jnp.bfloat16)
    return packed.reshape(count_dp, ROWS, factors.shape[1])


def on_device(hidden_in, out_grads, piece_of, owner_dp, owner_slot, sketch_in, sketch_out):
    count_dp = lax.axis_size("dp")
    count_fsdp = lax.axis_size("fsdp")
    width = sketch_in.shape[1]
    owned = count_dp // 2
    factors = project(hidden_in, out_grads, sketch_in, sketch_out)
    packed = pack_rows(factors, piece_of[0], owner_dp[0], owner_slot[0])
    got = lax.all_to_all(packed, "dp", split_axis=0, concat_axis=0, tiled=True)
    labels = got[:, CAP * SPAN : CAP * SPAN + CAP, 0].astype(jnp.int32)
    labels = jnp.repeat(labels, SPAN, axis=1)
    rows = got[:, : CAP * SPAN].reshape(count_dp * CAP * SPAN, 2 * width)
    hit = (labels.reshape(-1)[:, None] == 1 + jnp.arange(owned, dtype=jnp.int32)[None, :]).astype(jnp.bfloat16)
    spread = rows[:, :width][:, :, None] * hit[:, None, :]
    spread = spread.reshape(rows.shape[0], width * owned)
    features = lax.dot_general(spread, rows[:, width:], (((0,), (0,)), ((), ())), preferred_element_type=jnp.float32)
    features = features.astype(jnp.bfloat16)
    share = width // count_fsdp
    head = GR // width
    blocks = features.reshape(count_fsdp, share * owned, width)
    first = jnp.broadcast_to(features[: head * owned][None], (count_fsdp, head * owned, width))
    outgoing = jnp.concatenate([blocks, first], axis=1)
    mixed = lax.all_to_all(outgoing, "fsdp", split_axis=0, concat_axis=0, tiled=True)
    mixed = mixed.reshape(count_fsdp, share + head, owned, width)
    right = mixed[:, :share].transpose(0, 2, 1, 3).reshape(count_fsdp * owned, share * width)
    left = mixed[:, share:].transpose(0, 2, 1, 3).reshape(count_fsdp * owned, head * width)
    local_gram = lax.dot_general(left, right, (((0,), (0,)), ((), ())), preferred_element_type=jnp.float32)
    terms = lax.all_to_all(
        local_gram.reshape(count_dp, GR // count_dp, share * width), "dp", split_axis=0, concat_axis=0, tiled=True
    )
    scale_factor = 1.0 / math.sqrt(owned * count_dp * count_fsdp)
    return jnp.sum(terms, axis=0) * scale_factor


def solution(mesh):
    return jax.shard_map(
        on_device,
        mesh=mesh,
        in_specs=(
            P(("dp", "fsdp"), None),
            P(("dp", "fsdp"), None),
            P(("dp", "fsdp"), None),
            P(("dp", "fsdp"), None),
            P(("dp", "fsdp"), None),
            P("fsdp", None),
            P("fsdp", None),
        ),
        out_specs=P("dp", "fsdp"),
        check_vma=False,
    )
```

```python
import math

import jax
import jax.numpy as jnp
from jax import lax
from jax.experimental import pallas as pl
from jax.experimental.pallas import tpu as pltpu
from jax.sharding import PartitionSpec as P

CAP = 2
GR = 192
SPAN = 5
ROWS = 16
NX, NY, NZ = 4, 8, 6
ND = NY * NZ
GROUP = 16
EACH = 24
OWN = 24
SHIFT = 12
PARTS = 4
MESH = pl.DeviceIdType.MESH


def iota(shape, axis):
    return lax.broadcasted_iota(jnp.int32, shape, axis).astype(jnp.float32)


def one(mask, dtype=jnp.float32):
    return jnp.where(mask, 1.0, 0.0).astype(dtype)


def place_rows(piece_row, target_row, slot_row, select_ref, label_ref):
    pieces, tokens = target_row.shape[1], piece_row.shape[1]
    square = (pieces, pieces)
    down, along = iota(square, 0), iota(square, 1)
    diagonal = down == along

    def stand(row):
        return jnp.sum(jnp.where(diagonal, row, 0.0), axis=1, keepdims=True)

    target_col, slot_col = stand(target_row), stand(slot_row)
    before = jnp.where(target_col == 0.0, ND - 1.0, target_col - 1.0)
    met = jnp.sum(one(before == target_row), axis=1, keepdims=True)
    first = jnp.max(jnp.where(met == 0.0, target_col, -1.0), axis=0, keepdims=True)

    def order(target):
        ahead = target - first
        return jnp.where(ahead < 0.0, ahead + ND, ahead)

    same = target_col == target_row
    rank_col = jnp.sum(one(same & (along < down)), axis=1, keepdims=True)
    rank_row = jnp.sum(one(same & (down < along)), axis=0, keepdims=True)
    number = iota((pieces, tokens), 0)
    starts = jnp.sum(one(piece_row < number), axis=1, keepdims=True)
    base = order(target_col) * ROWS + rank_col * SPAN - starts
    place = iota((1, tokens), 1) + jnp.sum(jnp.where(piece_row == number, base, 0.0), axis=0, keepdims=True)
    label_place = order(target_row) * ROWS + CAP * SPAN + rank_row
    rows = select_ref.shape[0]
    select_ref[...] = one(iota((rows, tokens), 0) == place, jnp.bfloat16)
    label_at = one(iota((rows, pieces), 0) == label_place, jnp.bfloat16)
    labels = jnp.broadcast_to(slot_col + 1.0, (pieces, label_ref.shape[1])).astype(jnp.bfloat16)
    label_ref[...] = jnp.dot(label_at, labels, preferred_element_type=jnp.float32)


def gram_kernel(
    hidden_hbm, grads_hbm, in_hbm, out_hbm, piece_ref, target_ref, slot_ref, result_ref,
    hidden, grads, held, acc_in, acc_out, select, label_part, turn, spread_label, low, packed, owned_rows,
    feature, mixed, terms, gathered, load_sem, recv_sem, send_sem, edge_sem, inner_sem, swap_send, swap_recv,
):
    d, f = lax.axis_index("dp"), lax.axis_index("fsdp")
    p, y = d // NY, d % NY
    x, h, c = f // 4, (f // 2) % 2, f % 2
    wide_in, wide_out = in_hbm.shape[1], out_hbm.shape[1]
    step_rows = held.shape[1] // PARTS

    def name(x_, h_, c_):
        return x_ * 4 + h_ * 2 + c_

    east, west, far = (x + 1) % NX, (x + 3) % NX, (x + 2) % NX
    up_p, down_p = (p + 1) % NZ, (p + NZ - 1) % NZ
    up_h, down_h = (h + (p + 1) // NZ) % 2, (h + 1 - (p + NZ - 1) // NZ) % 2
    to_east, to_west, to_twin = (d, name(east, h, c)), (d, name(west, h, c)), (d, name(x, h, 1 - c))
    to_up = (up_p * NY + y, name(x, up_h, c))
    to_down = (down_p * NY + y, name(x, down_h, c))
    half = p // 3
    depth = p + half * (5 - 2 * p)
    to_inner = tuple((1 - half) * a + half * b for a, b in zip(to_up, to_down))
    to_outer = tuple((1 - half) * b + half * a for a, b in zip(to_up, to_down))

    def member(other):
        x_, c_ = (x + other // 4) % NX, (c + other % 2) % 2
        y_ = y + ((other // 2) % 2) * (1 - 2 * (y % 2))
        return (p * NY + y_, name(x_, h, c_)), name(x_, y_ % 2, c_)

    def prepare():
        place_rows(
            piece_ref[...].astype(jnp.float32), target_ref[...].astype(jnp.float32),
            slot_ref[...].astype(jnp.float32), select, label_part,
        )
        out_row, lane = iota(turn.shape, 0), iota(turn.shape, 1)
        wanted = jnp.where(out_row < 32.0, 2.0 * out_row, jnp.where(out_row < 64.0, 2.0 * out_row - 63.0, 0.0))
        turn[...] = one(lane == wanted, jnp.bfloat16)
        source = lax.broadcasted_iota(jnp.int32, spread_label.shape, 0)
        goal = lax.broadcasted_iota(jnp.int32, spread_label.shape, 1)
        inside = goal & (ROWS - 1)
        label_row = goal - inside + CAP * SPAN + jnp.where(inside >= SPAN, 1, 0)
        spread_label[...] = one((source == label_row) & (inside < CAP * SPAN), jnp.bfloat16)

    barrier = pltpu.get_barrier_semaphore()

    def greet(peer):
        pl.semaphore_signal(barrier, inc=1, device_id=peer, device_id_type=MESH)

    for peer in (to_east, to_west, to_twin, to_up, to_down):
        greet(peer)
    for other in range(1, GROUP):
        greet(member(other)[0])

    @pl.loop(1, ND)
    def _(j):
        greet(((d + j) % ND, f))
        greet(((d + j) % ND, name(x, 1 - h, c)))

    greet((d, name(x, 1 - h, c)))

    loads = (
        pltpu.make_async_copy(in_hbm, held.at[f, :, pl.ds(0, wide_in)], load_sem.at[0]),
        pltpu.make_async_copy(out_hbm, held.at[f, :, pl.ds(wide_in, wide_out)], load_sem.at[1]),
        pltpu.make_async_copy(grads_hbm, grads, load_sem.at[2]),
        pltpu.make_async_copy(hidden_hbm, hidden, load_sem.at[3]),
    )
    for load in loads:
        load.start()

    def move(shard, part, peer, sem):
        piece = held.at[shard, pl.ds(pl.multiple_of(part * step_rows, step_rows), step_rows), :]
        return pltpu.make_async_remote_copy(
            src_ref=piece, dst_ref=piece, send_sem=sem, recv_sem=recv_sem.at[shard, part],
            device_id=peer, device_id_type=MESH,
        )

    def send(shard, part, *peers):
        for peer in peers:
            move(shard, part, peer, send_sem).start()

    def arrived(shard, part):
        move(shard, part, to_twin, send_sem).wait_recv()

    prepare()
    pl.semaphore_wait(barrier, 5 + (GROUP - 1) + 2 * (ND - 1) + 1)
    loads[0].wait()
    loads[1].wait()

    for part in range(PARTS):

        @pl.when(depth == 0)
        def _():
            move(f, part, to_outer, edge_sem).start()

        send(f, part, to_east, to_west, to_twin)

    def pass_on(h_, part):
        for from_x, ahead, goes in ((west, to_east, part < PARTS // 2), (east, to_west, part >= PARTS // 2)):
            shard = name(from_x, h_, c)
            arrived(shard, part)
            if isinstance(goes, bool):
                if goes:
                    send(shard, part, ahead)
            else:
                pl.when(goes)(lambda: send(shard, part, ahead))
            send(shard, part, to_twin)

    across = name(x, 1 - h, c)

    @pl.loop(0, 2 * PARTS)
    def _(t):
        @pl.when(t < PARTS)
        def _():
            pass_on(h, t)

        part = t - 2 * depth

        @pl.when(jnp.logical_and(part >= 0, part < PARTS))
        def _():
            arrived(across, part)

            @pl.when(depth < 2)
            def _():
                move(across, part, to_inner, inner_sem).start()

            send(across, part, to_east, to_west, to_twin)

    acc_in[...] = jnp.zeros_like(acc_in)
    acc_out[...] = jnp.zeros_like(acc_out)
    nt = (((1,), (1,)), ((), ()))

    def use(shard):
        a = hidden[:, pl.ds(pl.multiple_of(shard * wide_in, 128), wide_in)]
        acc_in[...] += lax.dot_general(a, held[shard, :, :wide_in], nt, preferred_element_type=jnp.float32)
        b = grads[:, pl.ds(pl.multiple_of(shard * wide_out, 128), wide_out)]
        acc_out[...] += lax.dot_general(b, held[shard, :, wide_in:], nt, preferred_element_type=jnp.float32)

    def take(shard):
        for part in range(PARTS):
            arrived(shard, part)
        use(shard)

    def relay_far(h_):
        for part in range(PARTS):
            arrived(name(far, h_, c), part)
            send(name(far, h_, c), part, to_twin)

    relay_far(h)
    for part in range(PARTS):
        pass_on(1 - h, part)
    loads[2].wait()
    loads[3].wait()
    for x_ in (x, west, east, far):
        use(name(x_, h, c))
    for x_ in (x, west, east):
        use(name(x_, 1 - h, c))
    relay_far(1 - h)
    use(name(far, 1 - h, c))
    for h_ in (h, 1 - h):
        for x_ in (x, west, east, far):
            take(name(x_, h_, 1 - c))

    def drain(ref, count, sem):
        whole = ref.at[pl.ds(0, count)]
        pltpu.make_async_copy(whole, whole, sem).wait()

    low[:, :64] = acc_in[...].astype(low.dtype)
    low[:, 64:] = acc_out[...].astype(low.dtype)
    blocks = jnp.dot(select[...], low[...], preferred_element_type=jnp.float32) + label_part[...]
    packed[...] = blocks.astype(jnp.bfloat16).reshape(packed.shape)

    def post(src, dst, peer, phase):
        pltpu.make_async_remote_copy(
            src_ref=src, dst_ref=dst, send_sem=swap_send.at[phase], recv_sem=swap_recv.at[phase],
            device_id=peer, device_id_type=MESH,
        ).start()

    def keep(src, dst, phase):
        pltpu.make_async_copy(src, dst, swap_recv.at[phase]).start()

    keep(packed.at[SHIFT], owned_rows.at[SHIFT], 0)

    @pl.loop(1, EACH)
    def _(j):
        k = (SHIFT + j) % EACH
        post(packed.at[k], owned_rows.at[k], ((d + k + ND - SHIFT) % ND, f), 0)

    drain(owned_rows, EACH, swap_recv.at[0])

    rows = owned_rows[...].reshape(EACH * ROWS, 128)
    turned = lax.dot_general(turn[...], rows, nt, preferred_element_type=jnp.float32)
    label_rows = jnp.dot(turned[64:80].astype(jnp.bfloat16), spread_label[...], preferred_element_type=jnp.float32)
    hit = one(label_rows[:1] == iota((OWN, EACH * ROWS), 0) + 1.0)
    high = iota(rows.shape, 1) >= 64.0
    rows32 = rows.astype(jnp.float32)
    value_odd = jnp.where(high, rows32, 0.0).astype(jnp.bfloat16)
    value_even = jnp.where(high, 0.0, pltpu.roll(rows32, 64, 1)).astype(jnp.bfloat16)

    def expand(block):
        wide = block[:, None, :] * hit[None]
        return wide.reshape(32 * OWN, EACH * ROWS).astype(jnp.bfloat16)

    made = jnp.dot(expand(turned[:32]), value_even, preferred_element_type=jnp.float32)
    made += jnp.dot(expand(turned[32:64]), value_odd, preferred_element_type=jnp.float32)
    feature[...] = made.astype(jnp.bfloat16).reshape(feature.shape)

    here = name(x, y % 2, c)
    keep(feature.at[here], mixed.at[2 * here], 1)
    keep(feature.at[0], mixed.at[2 * here + 1], 1)
    for other in range(GROUP - 1, 0, -1):
        peer, columns = member(other)
        post(feature.at[columns], mixed.at[2 * here], peer, 1)
        post(feature.at[0], mixed.at[2 * here + 1], peer, 1)
    drain(mixed, 2 * GROUP, swap_recv.at[1])

    both = mixed[...].astype(jnp.float32).reshape(GROUP, 2, 2, OWN, 128)
    tn = (((0,), (0,)), ((), ()))

    def side(which, pair):
        return both[:, which, pair].reshape(GROUP * OWN, 128).astype(jnp.bfloat16)

    lefts = (side(1, 0), side(1, 1))
    tiles = []
    for pair in range(2):
        right = side(0, pair)
        top = lax.dot_general(lefts[0], right, tn, preferred_element_type=jnp.float32)
        low_part = lax.dot_general(lefts[1], right, tn, preferred_element_type=jnp.float32)
        tiles.append(jnp.concatenate([top, low_part[: GR - 128]], axis=0).reshape(GR // 8, 8, 128))
    upper = lax.broadcasted_iota(jnp.int32, tiles[0].shape, 1) < 4
    terms[:, 0] = jnp.where(upper, tiles[0], pltpu.roll(tiles[1], 4, 1))
    terms[:, 1] = jnp.where(upper, pltpu.roll(tiles[0], 4, 1), tiles[1])

    column = name(x, y % 2, c)
    mine = h * (ND // 2) + p * (NY // 2) + y // 2
    at_home = (y % 2) == h

    def term(o):
        return terms.at[o // 2, o % 2]

    @pl.when(at_home)
    def _():
        keep(term(d), gathered.at[mine], 2)

    @pl.when(jnp.logical_not(at_home))
    def _():
        post(term(d), gathered.at[mine], (d, column), 2)

    @pl.loop(1, ND)
    def _(j):
        o = (d + j) % ND
        post(term(o), gathered.at[mine], (o, column), 2)

    drain(gathered, ND, swap_recv.at[2])
    total = jnp.sum(gathered[...], axis=0) * (1.0 / math.sqrt(OWN * ND * GROUP))
    result_ref[:, :128] = total[:4]
    result_ref[:, 128:] = total[4:]

    drain(held, 14, send_sem)

    @pl.when(depth == 0)
    def _():
        drain(held, 1, edge_sem)

    @pl.when(depth < 2)
    def _():
        drain(held, 1, inner_sem)

    drain(packed, EACH - 1, swap_send.at[0])
    drain(mixed, 2 * (GROUP - 1), swap_send.at[1])

    @pl.when(at_home)
    def _():
        drain(gathered, ND - 1, swap_send.at[2])

    @pl.when(jnp.logical_not(at_home))
    def _():
        drain(gathered, ND, swap_send.at[2])


def on_device(hidden_in, out_grads, piece_of, owner_dp, owner_slot, sketch_in, sketch_out):
    rows = hidden_in.shape[0]
    width = sketch_in.shape[1]
    wide = sketch_in.shape[0] + sketch_out.shape[0]
    anywhere = pl.BlockSpec(memory_space=pl.ANY)
    vmem = pl.BlockSpec(memory_space=pltpu.VMEM)
    bf16, f32 = jnp.bfloat16, jnp.float32
    return pl.pallas_call(
        gram_kernel,
        out_shape=jax.ShapeDtypeStruct((GR // ND, 4096 // GROUP), f32),
        in_specs=[anywhere] * 4 + [vmem] * 3,
        out_specs=vmem,
        scratch_shapes=[
            pltpu.VMEM(hidden_in.shape, bf16),
            pltpu.VMEM(out_grads.shape, bf16),
            pltpu.VMEM((GROUP, width, wide), bf16),
            pltpu.VMEM((rows, width), f32),
            pltpu.VMEM((rows, width), f32),
            pltpu.VMEM((EACH * ROWS, rows), bf16),
            pltpu.VMEM((EACH * ROWS, 128), f32),
            pltpu.VMEM((80, 128), bf16),
            pltpu.VMEM((EACH * ROWS, EACH * ROWS), bf16),
            pltpu.VMEM((rows, 128), bf16),
            pltpu.VMEM((EACH, ROWS, 128), bf16),
            pltpu.VMEM((EACH, ROWS, 128), bf16),
            pltpu.VMEM((GROUP, 2 * OWN, 128), bf16),
            pltpu.VMEM((2 * GROUP, 2 * OWN, 128), bf16),
            pltpu.VMEM((GR // 8, 2, 8, 128), f32),
            pltpu.VMEM((ND, 8, 128), f32),
            pltpu.SemaphoreType.DMA((4,)),
            pltpu.SemaphoreType.DMA((GROUP, PARTS)),
            pltpu.SemaphoreType.DMA,
            pltpu.SemaphoreType.DMA,
            pltpu.SemaphoreType.DMA,
            pltpu.SemaphoreType.DMA((3,)),
            pltpu.SemaphoreType.DMA((3,)),
        ],
        compiler_params=pltpu.CompilerParams(collective_id=0, has_side_effects=True),
        name="gram",
    )(hidden_in, out_grads, sketch_in.T, sketch_out.T, piece_of, owner_dp, owner_slot)


def solution(mesh):
    return jax.shard_map(
        on_device,
        mesh=mesh,
        in_specs=(
            P(("dp", "fsdp"), None),
            P(("dp", "fsdp"), None),
            P(("dp", "fsdp"), None),
            P(("dp", "fsdp"), None),
            P(("dp", "fsdp"), None),
            P("fsdp", None),
            P("fsdp", None),
        ),
        out_specs=P("dp", "fsdp"),
        check_vma=False,
    )
```

```python
import math

import jax
import jax.numpy as jnp
from jax import lax
from jax.experimental import pallas as pl
from jax.experimental.pallas import tpu as pltpu
from jax.sharding import PartitionSpec as P

CAP = 2
GR = 192
SPAN = 5
ROWS = 16
NX, NY, NZ = 4, 8, 6
ND = NY * NZ
GROUP = 16
EACH = 24
OWN = 24
SHIFT = 12
ROUNDS = 7
PARTS = 4
MESH = pl.DeviceIdType.MESH


def iota(shape, axis):
    return lax.broadcasted_iota(jnp.int32, shape, axis).astype(jnp.float32)


def one(mask, dtype=jnp.float32):
    return jnp.where(mask, 1.0, 0.0).astype(dtype)


def place_rows(piece_row, target_row, slot_row, select_ref, label_ref):
    pieces, tokens = target_row.shape[1], piece_row.shape[1]
    square = (pieces, pieces)
    down, along = iota(square, 0), iota(square, 1)
    diagonal = down == along

    def stand(row):
        return jnp.sum(jnp.where(diagonal, row, 0.0), axis=1, keepdims=True)

    target_col, slot_col = stand(target_row), stand(slot_row)
    before = jnp.where(target_col == 0.0, ND - 1.0, target_col - 1.0)
    met = jnp.sum(one(before == target_row), axis=1, keepdims=True)
    first = jnp.max(jnp.where(met == 0.0, target_col, -1.0), axis=0, keepdims=True)

    def order(target):
        ahead = target - first
        return jnp.where(ahead < 0.0, ahead + ND, ahead)

    same = target_col == target_row
    rank_col = jnp.sum(one(same & (along < down)), axis=1, keepdims=True)
    rank_row = jnp.sum(one(same & (down < along)), axis=0, keepdims=True)
    number = iota((pieces, tokens), 0)
    starts = jnp.sum(one(piece_row < number), axis=1, keepdims=True)
    base = order(target_col) * ROWS + rank_col * SPAN - starts
    place = iota((1, tokens), 1) + jnp.sum(jnp.where(piece_row == number, base, 0.0), axis=0, keepdims=True)
    label_place = order(target_row) * ROWS + CAP * SPAN + rank_row
    rows = select_ref.shape[0]
    select_ref[...] = one(iota((rows, tokens), 0) == place, jnp.bfloat16)
    label_at = one(iota((rows, pieces), 0) == label_place, jnp.bfloat16)
    labels = jnp.broadcast_to(slot_col + 1.0, (pieces, label_ref.shape[1])).astype(jnp.bfloat16)
    label_ref[...] = jnp.dot(label_at, labels, preferred_element_type=jnp.float32)


def prepare_tables(piece_row, target_row, slot_row, select, label_part, turn, spread_label):
    place_rows(piece_row, target_row, slot_row, select, label_part)
    out_row, lane = iota(turn.shape, 0), iota(turn.shape, 1)
    wanted = jnp.where(out_row < 32.0, 2.0 * out_row, jnp.where(out_row < 64.0, 2.0 * out_row - 63.0, 0.0))
    turn[...] = one(lane == wanted, jnp.bfloat16)
    source = lax.broadcasted_iota(jnp.int32, spread_label.shape, 0)
    goal = lax.broadcasted_iota(jnp.int32, spread_label.shape, 1)
    inside = goal & (ROWS - 1)
    label_row = goal - inside + CAP * SPAN + jnp.where(inside >= SPAN, 1, 0)
    spread_label[...] = one((source == label_row) & (inside < CAP * SPAN), jnp.bfloat16)


def gram_kernel(
    hidden_hbm, grads_hbm, in_hbm, out_hbm, piece_ref, target_ref, slot_ref, result_ref,
    hidden, grads, held, acc_in, acc_out, select, label_part, turn, spread_label, low, packed, owned_rows,
    feature, mixed, terms, gathered, load_sem, recv_sem, send_sem, edge_sem, inner_sem, swap_send, swap_recv, round_sem,
):
    d, f = lax.axis_index("dp"), lax.axis_index("fsdp")
    p, y = d // NY, d % NY
    x, h, c = f // 4, (f // 2) % 2, f % 2
    side_y = y % 2
    wide_in, wide_out = in_hbm.shape[1], out_hbm.shape[1]
    step_rows = held.shape[1] // PARTS

    def name(x_, h_, c_):
        return x_ * 4 + h_ * 2 + c_

    def along_z(steps):
        z_ = (h * NZ + p + steps + 2 * NZ) % (2 * NZ)
        return ((z_ % NZ) * NY + y, name(x, z_ // NZ, c))

    def along_y(steps):
        return (p * NY + (y + steps + NY) % NY, f)

    east, west, far = (x + 1) % NX, (x + 3) % NX, (x + 2) % NX
    to_east, to_west, to_twin = (d, name(east, h, c)), (d, name(west, h, c)), (d, name(x, h, 1 - c))
    to_up, to_down = along_z(1), along_z(-1)
    to_pair = (p * NY + y + 1 - 2 * side_y, f)
    half = p // 3
    depth = p + half * (5 - 2 * p)
    to_inner = tuple((1 - half) * a + half * b for a, b in zip(to_up, to_down))
    to_outer = tuple((1 - half) * b + half * a for a, b in zip(to_up, to_down))

    def member(other):
        x_, c_ = (x + other // 4) % NX, (c + other % 2) % 2
        y_ = y + ((other // 2) % 2) * (1 - 2 * side_y)
        return (p * NY + y_, name(x_, h, c_)), name(x_, (y_ + p) % 2, c_)

    barrier = pltpu.get_barrier_semaphore()
    for peer in (to_east, to_west, to_twin, to_up, to_down, along_y(1), along_y(-1)):
        pl.semaphore_signal(barrier, inc=1, device_id=peer, device_id_type=MESH)

    loads = (
        pltpu.make_async_copy(in_hbm, held.at[f, :, pl.ds(0, wide_in)], load_sem.at[0]),
        pltpu.make_async_copy(out_hbm, held.at[f, :, pl.ds(wide_in, wide_out)], load_sem.at[1]),
        pltpu.make_async_copy(grads_hbm, grads, load_sem.at[2]),
        pltpu.make_async_copy(hidden_hbm, hidden, load_sem.at[3]),
    )
    for load in loads:
        load.start()

    circles = (
        (to_east, to_west, to_twin), (to_twin,), (along_y(1), along_y(-1)), (along_y(2), along_y(-2)),
        (to_up, to_down), (along_z(2), along_z(-2)), (along_z(3), along_z(-3)),
    )

    def tell(number):
        for peer in circles[number]:
            pl.semaphore_signal(round_sem.at[number], inc=1, device_id=peer, device_id_type=MESH)

    def hear(number):
        pl.semaphore_wait(round_sem.at[number], len(circles[number]))

    def hear_and_tell(number):
        hear(number)
        tell(number + 1)

    def move(shard, part, peer, sem):
        piece = held.at[shard, pl.ds(pl.multiple_of(part * step_rows, step_rows), step_rows), :]
        return pltpu.make_async_remote_copy(
            src_ref=piece, dst_ref=piece, send_sem=sem, recv_sem=recv_sem.at[shard, part],
            device_id=peer, device_id_type=MESH,
        )

    def send(shard, part, *peers):
        for peer in peers:
            move(shard, part, peer, send_sem).start()

    def arrived(shard, part):
        move(shard, part, to_twin, send_sem).wait_recv()

    def part_of(q):
        return (q % 2) * 2 + (q // 2) * (1 - 2 * side_y) + side_y

    pl.semaphore_wait(barrier, 7)
    loads[0].wait()
    loads[1].wait()

    for q in range(PARTS):

        @pl.when(depth == 0)
        def _():
            move(f, part_of(q), to_outer, edge_sem).start()

        if q < 3:
            send(f, part_of(q), to_east, to_west)
        send(f, part_of(q), to_twin)
    tell(0)

    def near(h_, q):
        part = part_of(q)
        first, second = name(west, h_, c), name(east, h_, c)
        arrived(first, part)
        if q == 0:
            send(first, part, to_east)
        if q == 1:
            send(first, part, to_pair)
        send(first, part, to_twin)
        arrived(second, part)
        if q == 1:
            send(second, part, to_west, to_pair)
        send(second, part, to_twin)

    def remote(h_, q):
        shard, part = name(far, h_, c), part_of(q)
        arrived(shard, part)
        if q < 2:
            send(shard, part, to_pair)
        send(shard, part, to_twin)

    across = name(x, 1 - h, c)

    for t in range(2 * PARTS):
        if t < 3:
            near(h, t)
        q = t - 2 * depth

        @pl.when(jnp.logical_and(q >= 0, q < PARTS))
        def _():
            part = part_of(q)
            arrived(across, part)

            @pl.when(depth < 2)
            def _():
                move(across, part, to_inner, inner_sem).start()

            @pl.when(q < 3)
            def _():
                send(across, part, to_east, to_west)

            send(across, part, to_twin)

        if t == 3:
            hear_and_tell(0)
        if t == 5:
            hear_and_tell(1)

    def use(shard):
        a = hidden[:, pl.ds(pl.multiple_of(shard * wide_in, 128), wide_in)]
        acc_in[...] += lax.dot_general(a, held[shard, :, :wide_in], nt, preferred_element_type=jnp.float32)
        b = grads[:, pl.ds(pl.multiple_of(shard * wide_out, 128), wide_out)]
        acc_out[...] += lax.dot_general(b, held[shard, :, wide_in:], nt, preferred_element_type=jnp.float32)

    def take(shard):
        for part in range(PARTS):
            arrived(shard, part)
        use(shard)

    nt = (((1,), (1,)), ((), ()))
    acc_in[...] = jnp.zeros_like(acc_in)
    acc_out[...] = jnp.zeros_like(acc_out)
    remote(h, 0)
    remote(h, 1)
    hear_and_tell(2)
    near(1 - h, 0)
    near(h, 3)
    hear_and_tell(3)
    near(1 - h, 1)
    remote(h, 2)
    remote(h, 3)
    near(1 - h, 2)
    hear_and_tell(4)
    remote(1 - h, 0)
    remote(1 - h, 1)
    prepare_tables(
        piece_ref[...].astype(jnp.float32), target_ref[...].astype(jnp.float32), slot_ref[...].astype(jnp.float32),
        select, label_part, turn, spread_label,
    )
    loads[2].wait()
    loads[3].wait()
    for x_ in (x, west, east, far):
        use(name(x_, h, c))
    hear_and_tell(5)
    near(1 - h, 3)
    remote(1 - h, 2)
    remote(1 - h, 3)
    for x_ in (x, west, east, far):
        take(name(x_, h, 1 - c))
    for x_ in (x, west, east, far):
        use(name(x_, 1 - h, c))
    for x_ in (x, west, east, far):
        take(name(x_, 1 - h, 1 - c))
    hear(6)

    def drain(ref, count, sem):
        whole = ref.at[pl.ds(0, count)]
        pltpu.make_async_copy(whole, whole, sem).wait()

    low[:, :64] = acc_in[...].astype(low.dtype)
    low[:, 64:] = acc_out[...].astype(low.dtype)
    blocks = jnp.dot(select[...], low[...], preferred_element_type=jnp.float32) + label_part[...]
    packed[...] = blocks.astype(jnp.bfloat16).reshape(packed.shape)

    def post(src, dst, peer, phase):
        pltpu.make_async_remote_copy(
            src_ref=src, dst_ref=dst, send_sem=swap_send.at[phase], recv_sem=swap_recv.at[phase],
            device_id=peer, device_id_type=MESH,
        ).start()

    def keep(src, dst, phase):
        pltpu.make_async_copy(src, dst, swap_recv.at[phase]).start()

    keep(packed.at[SHIFT], owned_rows.at[SHIFT], 0)

    @pl.loop(1, EACH)
    def _(j):
        k = (SHIFT + j) % EACH
        post(packed.at[k], owned_rows.at[k], ((d + k + ND - SHIFT) % ND, f), 0)

    drain(owned_rows, EACH, swap_recv.at[0])

    rows = owned_rows[...].reshape(EACH * ROWS, 128)
    turned = lax.dot_general(turn[...], rows, nt, preferred_element_type=jnp.float32)
    label_rows = jnp.dot(turned[64:80].astype(jnp.bfloat16), spread_label[...], preferred_element_type=jnp.float32)
    hit = one(label_rows[:1] == iota((OWN, EACH * ROWS), 0) + 1.0)
    high = iota(rows.shape, 1) >= 64.0
    rows32 = rows.astype(jnp.float32)
    value_odd = jnp.where(high, rows32, 0.0).astype(jnp.bfloat16)
    value_even = jnp.where(high, 0.0, pltpu.roll(rows32, 64, 1)).astype(jnp.bfloat16)

    def expand(block):
        wide = block[:, None, :] * hit[None]
        return wide.reshape(32 * OWN, EACH * ROWS).astype(jnp.bfloat16)

    made = jnp.dot(expand(turned[:32]), value_even, preferred_element_type=jnp.float32)
    made += jnp.dot(expand(turned[32:64]), value_odd, preferred_element_type=jnp.float32)
    feature[...] = made.astype(jnp.bfloat16).reshape(feature.shape)

    here = name(x, (y + p) % 2, c)
    keep(feature.at[here], mixed.at[2 * here], 1)
    keep(feature.at[0], mixed.at[2 * here + 1], 1)
    for other in range(GROUP - 1, 0, -1):
        peer, columns = member(other)
        post(feature.at[columns], mixed.at[2 * here], peer, 1)
        post(feature.at[0], mixed.at[2 * here + 1], peer, 1)
    drain(mixed, 2 * GROUP, swap_recv.at[1])

    both = mixed[...].astype(jnp.float32).reshape(GROUP, 2, 2, OWN, 128)
    tn = (((0,), (0,)), ((), ()))

    def side(which, pair):
        return both[:, which, pair].reshape(GROUP * OWN, 128).astype(jnp.bfloat16)

    lefts = (side(1, 0), side(1, 1))
    tiles = []
    for pair in range(2):
        right = side(0, pair)
        top = lax.dot_general(lefts[0], right, tn, preferred_element_type=jnp.float32)
        low_part = lax.dot_general(lefts[1], right, tn, preferred_element_type=jnp.float32)
        tiles.append(jnp.concatenate([top, low_part[: GR - 128]], axis=0).reshape(GR // 8, 8, 128))
    upper = lax.broadcasted_iota(jnp.int32, tiles[0].shape, 1) < 4
    terms[:, 0] = jnp.where(upper, tiles[0], pltpu.roll(tiles[1], 4, 1)).astype(terms.dtype)
    terms[:, 1] = jnp.where(upper, pltpu.roll(tiles[0], 4, 1), tiles[1]).astype(terms.dtype)

    column = name(x, (y + p) % 2, c)
    mine = h * (ND // 2) + p * (NY // 2) + y // 2
    at_home = ((y + p) % 2) == h

    def term(o):
        return terms.at[o // 2, o % 2]

    @pl.when(at_home)
    def _():
        keep(term(d), gathered.at[mine], 2)

    @pl.when(jnp.logical_not(at_home))
    def _():
        post(term(d), gathered.at[mine], (d, column), 2)

    @pl.loop(1, ND)
    def _(j):
        o = (d + j) % ND
        post(term(o), gathered.at[mine], (o, column), 2)

    drain(gathered, ND, swap_recv.at[2])
    total = jnp.sum(gathered[...].astype(jnp.float32), axis=0)
    result_ref[:, :128] = total[:4]
    result_ref[:, 128:] = total[4:]

    drain(held, 14, send_sem)

    @pl.when(depth == 0)
    def _():
        drain(held, 1, edge_sem)

    @pl.when(depth < 2)
    def _():
        drain(held, 1, inner_sem)

    drain(packed, EACH - 1, swap_send.at[0])
    drain(mixed, 2 * (GROUP - 1), swap_send.at[1])

    @pl.when(at_home)
    def _():
        drain(gathered, ND - 1, swap_send.at[2])

    @pl.when(jnp.logical_not(at_home))
    def _():
        drain(gathered, ND, swap_send.at[2])


def on_device(hidden_in, out_grads, piece_of, owner_dp, owner_slot, sketch_in, sketch_out):
    rows = hidden_in.shape[0]
    width = sketch_in.shape[1]
    wide = sketch_in.shape[0] + sketch_out.shape[0]
    anywhere = pl.BlockSpec(memory_space=pl.ANY)
    vmem = pl.BlockSpec(memory_space=pltpu.VMEM)
    bf16, f32 = jnp.bfloat16, jnp.float32
    total = pl.pallas_call(
        gram_kernel,
        out_shape=jax.ShapeDtypeStruct((GR // ND, 4096 // GROUP), f32),
        in_specs=[anywhere] * 4 + [vmem] * 3,
        out_specs=vmem,
        scratch_shapes=[
            pltpu.VMEM(hidden_in.shape, bf16),
            pltpu.VMEM(out_grads.shape, bf16),
            pltpu.VMEM((GROUP, width, wide), bf16),
            pltpu.VMEM((rows, width), f32),
            pltpu.VMEM((rows, width), f32),
            pltpu.VMEM((EACH * ROWS, rows), bf16),
            pltpu.VMEM((EACH * ROWS, 128), f32),
            pltpu.VMEM((80, 128), bf16),
            pltpu.VMEM((EACH * ROWS, EACH * ROWS), bf16),
            pltpu.VMEM((rows, 128), bf16),
            pltpu.VMEM((EACH, ROWS, 128), bf16),
            pltpu.VMEM((EACH, ROWS, 128), bf16),
            pltpu.VMEM((GROUP, 2 * OWN, 128), bf16),
            pltpu.VMEM((2 * GROUP, 2 * OWN, 128), bf16),
            pltpu.VMEM((GR // 8, 2, 8, 128), bf16),
            pltpu.VMEM((ND, 8, 128), bf16),
            pltpu.SemaphoreType.DMA((4,)),
            pltpu.SemaphoreType.DMA((GROUP, PARTS)),
            pltpu.SemaphoreType.DMA,
            pltpu.SemaphoreType.DMA,
            pltpu.SemaphoreType.DMA,
            pltpu.SemaphoreType.DMA((3,)),
            pltpu.SemaphoreType.DMA((3,)),
            pltpu.SemaphoreType.REGULAR((ROUNDS,)),
        ],
        compiler_params=pltpu.CompilerParams(collective_id=0, has_side_effects=True),
        name="gram",
    )(hidden_in, out_grads, sketch_in.T, sketch_out.T, piece_of, owner_dp, owner_slot)
    return total * (1.0 / math.sqrt(OWN * ND * GROUP))


def solution(mesh):
    return jax.shard_map(
        on_device,
        mesh=mesh,
        in_specs=(
            P(("dp", "fsdp"), None),
            P(("dp", "fsdp"), None),
            P(("dp", "fsdp"), None),
            P(("dp", "fsdp"), None),
            P(("dp", "fsdp"), None),
            P("fsdp", None),
            P("fsdp", None),
        ),
        out_specs=P("dp", "fsdp"),
        check_vma=False,
    )
```

```python
import math

import jax
import jax.numpy as jnp
from jax import lax
from jax.experimental import pallas as pl
from jax.experimental.pallas import tpu as pltpu
from jax.sharding import PartitionSpec as P

CAP = 2
GR = 192
SPAN = 5
ROWS = 16
NX, NY, NZ = 4, 8, 6
ND = NY * NZ
GROUP = 16
EACH = 24
OWN = 24
SHIFT = 12
ROUNDS = 7
PARTS = 4
MESH = pl.DeviceIdType.MESH


def iota(shape, axis):
    return lax.broadcasted_iota(jnp.int32, shape, axis).astype(jnp.float32)


def one(mask, dtype=jnp.float32):
    return jnp.where(mask, 1.0, 0.0).astype(dtype)


def place_rows(piece_row, target_row, slot_row, select_ref, label_ref):
    pieces, tokens = target_row.shape[1], piece_row.shape[1]
    square = (pieces, pieces)
    down, along = iota(square, 0), iota(square, 1)
    diagonal = down == along

    def stand(row):
        return jnp.sum(jnp.where(diagonal, row, 0.0), axis=1, keepdims=True)

    target_col, slot_col = stand(target_row), stand(slot_row)
    before = jnp.where(target_col == 0.0, ND - 1.0, target_col - 1.0)
    met = jnp.sum(one(before == target_row), axis=1, keepdims=True)
    first = jnp.max(jnp.where(met == 0.0, target_col, -1.0), axis=0, keepdims=True)

    def order(target):
        ahead = target - first
        return jnp.where(ahead < 0.0, ahead + ND, ahead)

    same = target_col == target_row
    rank_col = jnp.sum(one(same & (along < down)), axis=1, keepdims=True)
    rank_row = jnp.sum(one(same & (down < along)), axis=0, keepdims=True)
    number = iota((pieces, tokens), 0)
    starts = jnp.sum(one(piece_row < number), axis=1, keepdims=True)
    base = order(target_col) * ROWS + rank_col * SPAN - starts
    place = iota((1, tokens), 1) + jnp.sum(jnp.where(piece_row == number, base, 0.0), axis=0, keepdims=True)
    label_place = order(target_row) * ROWS + CAP * SPAN + rank_row
    rows = select_ref.shape[0]
    select_ref[...] = one(iota((rows, tokens), 0) == place, jnp.bfloat16)
    label_at = one(iota((rows, pieces), 0) == label_place, jnp.bfloat16)
    labels = jnp.broadcast_to(slot_col + 1.0, (pieces, label_ref.shape[1])).astype(jnp.bfloat16)
    label_ref[...] = jnp.dot(label_at, labels, preferred_element_type=jnp.float32)


def prepare_tables(piece_row, target_row, slot_row, select, label_part, turn, spread_label):
    place_rows(piece_row, target_row, slot_row, select, label_part)
    out_row, lane = iota(turn.shape, 0), iota(turn.shape, 1)
    wanted = jnp.where(out_row < 32.0, 2.0 * out_row, jnp.where(out_row < 64.0, 2.0 * out_row - 63.0, 0.0))
    turn[...] = one(lane == wanted, jnp.bfloat16)
    source = lax.broadcasted_iota(jnp.int32, spread_label.shape, 0)
    goal = lax.broadcasted_iota(jnp.int32, spread_label.shape, 1)
    inside = goal & (ROWS - 1)
    label_row = goal - inside + CAP * SPAN + jnp.where(inside >= SPAN, 1, 0)
    spread_label[...] = one((source == label_row) & (inside < CAP * SPAN), jnp.bfloat16)


def gram_kernel(
    hidden_hbm, grads_hbm, in_hbm, out_hbm, piece_hbm, target_hbm, slot_hbm, result_ref,
    piece_ref, target_ref, slot_ref, hidden, grads, held, acc_in, acc_out, select, label_part, turn, spread_label, low, packed, owned_rows,
    feature, mixed, terms, gathered, load_sem, recv_sem, send_sem, edge_sem, inner_sem, swap_send, swap_recv, round_sem,
):
    d, f = lax.axis_index("dp"), lax.axis_index("fsdp")
    p, y = d // NY, d % NY
    x, h, c = f // 4, (f // 2) % 2, f % 2
    wide_in, wide_out = in_hbm.shape[1], out_hbm.shape[1]
    step_rows = held.shape[1] // PARTS

    def name(x_, h_, c_):
        return x_ * 4 + h_ * 2 + c_

    def along_z(steps):
        z_ = (h * NZ + p + steps + 2 * NZ) % (2 * NZ)
        return ((z_ % NZ) * NY + y, name(x, z_ // NZ, c))

    def along_y(steps):
        return (p * NY + (y + steps + NY) % NY, f)

    east, west, far = (x + 1) % NX, (x + 3) % NX, (x + 2) % NX
    to_east, to_west, to_twin = (d, name(east, h, c)), (d, name(west, h, c)), (d, name(x, h, 1 - c))
    to_up, to_down = along_z(1), along_z(-1)
    to_far = (d, name(far, h, c))
    half = p // 3
    depth = p + half * (5 - 2 * p)
    to_inner = tuple((1 - half) * a + half * b for a, b in zip(to_up, to_down))
    to_outer = tuple((1 - half) * b + half * a for a, b in zip(to_up, to_down))

    def member(other):
        x_, c_ = (x + other // 4) % NX, (c + other % 2) % 2
        y_ = y + ((other // 2) % 2) * (1 - 2 * (y % 2))
        return (p * NY + y_, name(x_, h, c_)), name(x_, (y_ + p) % 2, c_)

    barrier = pltpu.get_barrier_semaphore()
    for peer in (to_east, to_west, to_far, to_twin, to_up, to_down, along_y(1), along_y(-1)):
        pl.semaphore_signal(barrier, inc=1, device_id=peer, device_id_type=MESH)

    loads = (
        pltpu.make_async_copy(in_hbm, held.at[f, :, pl.ds(0, wide_in)], load_sem.at[0]),
        pltpu.make_async_copy(out_hbm, held.at[f, :, pl.ds(wide_in, wide_out)], load_sem.at[1]),
        pltpu.make_async_copy(grads_hbm, grads, load_sem.at[2]),
        pltpu.make_async_copy(hidden_hbm, hidden, load_sem.at[3]),
        pltpu.make_async_copy(piece_hbm, piece_ref, load_sem.at[4]),
        pltpu.make_async_copy(target_hbm, target_ref, load_sem.at[5]),
        pltpu.make_async_copy(slot_hbm, slot_ref, load_sem.at[6]),
    )

    circles = (
        (to_east, to_west, to_twin), (to_twin,), (along_y(1), along_y(-1)), (along_y(2), along_y(-2)),
        (to_up, to_down), (along_z(2), along_z(-2)), (along_z(3), along_z(-3)),
    )

    def tell(number):
        for peer in circles[number]:
            pl.semaphore_signal(round_sem.at[number], inc=1, device_id=peer, device_id_type=MESH)

    def hear(number):
        pl.semaphore_wait(round_sem.at[number], len(circles[number]))

    def hear_and_tell(number):
        hear(number)
        tell(number + 1)

    def move(shard, part, peer, sem):
        piece = held.at[shard, pl.ds(pl.multiple_of(part * step_rows, step_rows), step_rows), :]
        return pltpu.make_async_remote_copy(
            src_ref=piece, dst_ref=piece, send_sem=sem, recv_sem=recv_sem.at[shard, part],
            device_id=peer, device_id_type=MESH,
        )

    def send(shard, part, *peers):
        for peer in peers:
            move(shard, part, peer, send_sem).start()

    def first_send(part, peer, sem):
        rows_ = pl.ds(part * step_rows, step_rows)
        for ref, lanes in ((in_hbm, pl.ds(0, wide_in)), (out_hbm, pl.ds(wide_in, wide_out))):
            pltpu.make_async_remote_copy(
                src_ref=ref.at[rows_, :], dst_ref=held.at[f, rows_, lanes], send_sem=sem, recv_sem=recv_sem.at[f, part],
                device_id=peer, device_id_type=MESH,
            ).start()

    def arrived(shard, part):
        move(shard, part, to_twin, send_sem).wait_recv()

    pl.semaphore_wait(barrier, 8)
    for q in range(PARTS):

        @pl.when(depth == 0)
        def _():
            first_send(q, to_outer, edge_sem)

        for peer in (to_east, to_west, to_far, to_twin):
            first_send(q, peer, send_sem)
    tell(0)
    for load in loads:
        load.start()

    def near(h_, q):
        part = q
        first, second = name(west, h_, c), name(east, h_, c)
        for shard in (first, second):
            arrived(shard, part)
            send(shard, part, to_twin)

    def remote(h_, q):
        shard, part = name(far, h_, c), q
        arrived(shard, part)
        send(shard, part, to_twin)

    across = name(x, 1 - h, c)

    for t in range(2 * PARTS):
        if t < 4:
            near(h, t)
        q = t - 2 * depth

        @pl.when(jnp.logical_and(q >= 0, q < PARTS))
        def _():
            part = q
            arrived(across, part)

            @pl.when(depth < 2)
            def _():
                move(across, part, to_inner, inner_sem).start()

            send(across, part, to_east, to_west, to_far, to_twin)

        if t < ROUNDS - 1:
            hear_and_tell(t)

    def use(shard):
        a = hidden[:, pl.ds(pl.multiple_of(shard * wide_in, 128), wide_in)]
        acc_in[...] += lax.dot_general(a, held[shard, :, :wide_in], nt, preferred_element_type=jnp.float32)
        b = grads[:, pl.ds(pl.multiple_of(shard * wide_out, 128), wide_out)]
        acc_out[...] += lax.dot_general(b, held[shard, :, wide_in:], nt, preferred_element_type=jnp.float32)

    def take(shard):
        for part in range(PARTS):
            arrived(shard, part)
        use(shard)

    nt = (((1,), (1,)), ((), ()))
    acc_in[...] = jnp.zeros_like(acc_in)
    acc_out[...] = jnp.zeros_like(acc_out)
    for load in loads[4:]:
        load.wait()
    prepare_tables(
        piece_ref[...].astype(jnp.float32), target_ref[...].astype(jnp.float32), slot_ref[...].astype(jnp.float32),
        select, label_part, turn, spread_label,
    )
    for load in loads[:4]:
        load.wait()
    remote(h, 0)
    remote(h, 1)
    remote(h, 2)
    remote(h, 3)
    near(1 - h, 0)
    near(1 - h, 1)
    near(1 - h, 2)
    near(1 - h, 3)
    for x_ in (x, west, east, far):
        use(name(x_, h, c))
    for x_ in (x, west, east, far):
        take(name(x_, h, 1 - c))
    for x_ in (x, west, east):
        use(name(x_, 1 - h, c))
    remote(1 - h, 0)
    remote(1 - h, 1)
    remote(1 - h, 2)
    remote(1 - h, 3)
    for x_ in (x, west, east):
        take(name(x_, 1 - h, 1 - c))
    use(name(far, 1 - h, c))
    take(name(far, 1 - h, 1 - c))
    hear(6)

    def drain(ref, count, sem):
        whole = ref.at[pl.ds(0, count)]
        pltpu.make_async_copy(whole, whole, sem).wait()

    low[:, :64] = acc_in[...].astype(low.dtype)
    low[:, 64:] = acc_out[...].astype(low.dtype)
    blocks = jnp.dot(select[...], low[...], preferred_element_type=jnp.float32) + label_part[...]
    packed[...] = blocks.astype(jnp.bfloat16).reshape(packed.shape)

    def post(src, dst, peer, phase):
        pltpu.make_async_remote_copy(
            src_ref=src, dst_ref=dst, send_sem=swap_send.at[phase], recv_sem=swap_recv.at[phase],
            device_id=peer, device_id_type=MESH,
        ).start()

    def keep(src, dst, phase):
        pltpu.make_async_copy(src, dst, swap_recv.at[phase]).start()

    keep(packed.at[SHIFT], owned_rows.at[SHIFT], 0)

    for k in sorted(range(EACH), key=lambda k: -abs(k - SHIFT))[:-1]:
        post(packed.at[k], owned_rows.at[k], ((d + k + ND - SHIFT) % ND, f), 0)

    drain(owned_rows, EACH, swap_recv.at[0])

    rows = owned_rows[...].reshape(EACH * ROWS, 128)
    turned = lax.dot_general(turn[...], rows, nt, preferred_element_type=jnp.float32)
    label_rows = jnp.dot(turned[64:80].astype(jnp.bfloat16), spread_label[...], preferred_element_type=jnp.float32)
    hit = one(label_rows[:1] == iota((OWN, EACH * ROWS), 0) + 1.0)
    high = iota(rows.shape, 1) >= 64.0
    rows32 = rows.astype(jnp.float32)
    value_odd = jnp.where(high, rows32, 0.0).astype(jnp.bfloat16)
    value_even = jnp.where(high, 0.0, pltpu.roll(rows32, 64, 1)).astype(jnp.bfloat16)

    def expand(block):
        wide = block[:, None, :] * hit[None]
        return wide.reshape(32 * OWN, EACH * ROWS).astype(jnp.bfloat16)

    made = jnp.dot(expand(turned[:32]), value_even, preferred_element_type=jnp.float32)
    made += jnp.dot(expand(turned[32:64]), value_odd, preferred_element_type=jnp.float32)
    feature[...] = made.astype(jnp.bfloat16).reshape(feature.shape)

    here = name(x, (y + p) % 2, c)
    keep(feature.at[here], mixed.at[2 * here], 1)
    keep(feature.at[0], mixed.at[2 * here + 1], 1)
    for other in range(GROUP - 1, 0, -1):
        peer, columns = member(other)
        post(feature.at[columns], mixed.at[2 * here], peer, 1)
        post(feature.at[0], mixed.at[2 * here + 1], peer, 1)
    drain(mixed, 2 * GROUP, swap_recv.at[1])

    both = mixed[...].astype(jnp.float32).reshape(GROUP, 2, 2, OWN, 128)
    tn = (((0,), (0,)), ((), ()))

    def side(which, pair):
        return both[:, which, pair].reshape(GROUP * OWN, 128).astype(jnp.bfloat16)

    lefts = (side(1, 0), side(1, 1))
    tiles = []
    for pair in range(2):
        right = side(0, pair)
        top = lax.dot_general(lefts[0], right, tn, preferred_element_type=jnp.float32)
        low_part = lax.dot_general(lefts[1], right, tn, preferred_element_type=jnp.float32)
        tiles.append(jnp.concatenate([top, low_part[: GR - 128]], axis=0).reshape(GR // 8, 8, 128))
    upper = lax.broadcasted_iota(jnp.int32, tiles[0].shape, 1) < 4
    terms[:, 0] = jnp.where(upper, tiles[0], pltpu.roll(tiles[1], 4, 1)).astype(terms.dtype)
    terms[:, 1] = jnp.where(upper, pltpu.roll(tiles[0], 4, 1), tiles[1]).astype(terms.dtype)

    column = name(x, (y + p) % 2, c)
    mine = h * (ND // 2) + p * (NY // 2) + y // 2
    at_home = ((y + p) % 2) == h

    def term(o):
        return terms.at[o // 2, o % 2]

    start = d + jnp.where(at_home, ND // 2, 0)

    @pl.loop(0, ND)
    def _(j):
        o = (start + j) % ND
        here_too = jnp.logical_and(at_home, o == d)

        @pl.when(here_too)
        def _():
            keep(term(o), gathered.at[mine], 2)

        @pl.when(jnp.logical_not(here_too))
        def _():
            post(term(o), gathered.at[mine], (o, column), 2)

    drain(gathered, ND, swap_recv.at[2])
    total = jnp.sum(gathered[...].astype(jnp.float32), axis=0)
    result_ref[:, :128] = total[:4]
    result_ref[:, 128:] = total[4:]

    drain(held, 14, send_sem)

    @pl.when(depth == 0)
    def _():
        drain(held, 1, edge_sem)

    @pl.when(depth < 2)
    def _():
        drain(held, 1, inner_sem)

    drain(packed, EACH - 1, swap_send.at[0])
    drain(mixed, 2 * (GROUP - 1), swap_send.at[1])

    @pl.when(at_home)
    def _():
        drain(gathered, ND - 1, swap_send.at[2])

    @pl.when(jnp.logical_not(at_home))
    def _():
        drain(gathered, ND, swap_send.at[2])


def on_device(hidden_in, out_grads, piece_of, owner_dp, owner_slot, sketch_in, sketch_out):
    rows = hidden_in.shape[0]
    width = sketch_in.shape[1]
    wide = sketch_in.shape[0] + sketch_out.shape[0]
    anywhere = pl.BlockSpec(memory_space=pl.ANY)
    vmem = pl.BlockSpec(memory_space=pltpu.VMEM)
    bf16, f32 = jnp.bfloat16, jnp.float32
    total = pl.pallas_call(
        gram_kernel,
        out_shape=jax.ShapeDtypeStruct((GR // ND, 4096 // GROUP), f32),
        in_specs=[anywhere] * 7,
        out_specs=vmem,
        scratch_shapes=[
            pltpu.VMEM(piece_of.shape, jnp.int32),
            pltpu.VMEM(owner_dp.shape, jnp.int32),
            pltpu.VMEM(owner_slot.shape, jnp.int32),
            pltpu.VMEM(hidden_in.shape, bf16),
            pltpu.VMEM(out_grads.shape, bf16),
            pltpu.VMEM((GROUP, width, wide), bf16),
            pltpu.VMEM((rows, width), f32),
            pltpu.VMEM((rows, width), f32),
            pltpu.VMEM((EACH * ROWS, rows), bf16),
            pltpu.VMEM((EACH * ROWS, 128), f32),
            pltpu.VMEM((80, 128), bf16),
            pltpu.VMEM((EACH * ROWS, EACH * ROWS), bf16),
            pltpu.VMEM((rows, 128), bf16),
            pltpu.VMEM((EACH, ROWS, 128), bf16),
            pltpu.VMEM((EACH, ROWS, 128), bf16),
            pltpu.VMEM((GROUP, 2 * OWN, 128), bf16),
            pltpu.VMEM((2 * GROUP, 2 * OWN, 128), bf16),
            pltpu.VMEM((GR // 8, 2, 8, 128), bf16),
            pltpu.VMEM((ND, 8, 128), bf16),
            pltpu.SemaphoreType.DMA((7,)),
            pltpu.SemaphoreType.DMA((GROUP, PARTS)),
            pltpu.SemaphoreType.DMA,
            pltpu.SemaphoreType.DMA,
            pltpu.SemaphoreType.DMA,
            pltpu.SemaphoreType.DMA((3,)),
            pltpu.SemaphoreType.DMA((3,)),
            pltpu.SemaphoreType.REGULAR((ROUNDS,)),
        ],
        compiler_params=pltpu.CompilerParams(collective_id=0, has_side_effects=True),
        name="gram",
    )(hidden_in, out_grads, sketch_in.T, sketch_out.T, piece_of, owner_dp, owner_slot)
    return total * (1.0 / math.sqrt(OWN * ND * GROUP))


def solution(mesh):
    return jax.shard_map(
        on_device,
        mesh=mesh,
        in_specs=(
            P(("dp", "fsdp"), None),
            P(("dp", "fsdp"), None),
            P(("dp", "fsdp"), None),
            P(("dp", "fsdp"), None),
            P(("dp", "fsdp"), None),
            P("fsdp", None),
            P("fsdp", None),
        ),
        out_specs=P("dp", "fsdp"),
        check_vma=False,
    )
```

```python
import math

import jax
import jax.numpy as jnp
from jax import lax
from jax.experimental import pallas as pl
from jax.experimental.pallas import tpu as pltpu
from jax.sharding import PartitionSpec as P

CAP = 2
GR = 192
SPAN = 5
ROWS = 16
NX, NY, NZ = 4, 8, 6
ND = NY * NZ
GROUP = 16
EACH = 24
OWN = 24
SHIFT = 12
ROUNDS = 7
PARTS = 4
MESH = pl.DeviceIdType.MESH


def iota(shape, axis):
    return lax.broadcasted_iota(jnp.int32, shape, axis).astype(jnp.float32)


def one(mask, dtype=jnp.float32):
    return jnp.where(mask, 1.0, 0.0).astype(dtype)


def place_rows(piece_row, target_row, slot_row, select_ref, label_ref):
    pieces, tokens = target_row.shape[1], piece_row.shape[1]
    square = (pieces, pieces)
    down, along = iota(square, 0), iota(square, 1)
    diagonal = down == along

    def stand(row):
        return jnp.sum(jnp.where(diagonal, row, 0.0), axis=1, keepdims=True)

    target_col, slot_col = stand(target_row), stand(slot_row)
    before = jnp.where(target_col == 0.0, ND - 1.0, target_col - 1.0)
    met = jnp.sum(one(before == target_row), axis=1, keepdims=True)
    first = jnp.max(jnp.where(met == 0.0, target_col, -1.0), axis=0, keepdims=True)

    def order(target):
        ahead = target - first
        return jnp.where(ahead < 0.0, ahead + ND, ahead)

    same = target_col == target_row
    rank_col = jnp.sum(one(same & (along < down)), axis=1, keepdims=True)
    rank_row = jnp.sum(one(same & (down < along)), axis=0, keepdims=True)
    number = iota((pieces, tokens), 0)
    starts = jnp.sum(one(piece_row < number), axis=1, keepdims=True)
    base = order(target_col) * ROWS + rank_col * SPAN - starts
    place = iota((1, tokens), 1) + jnp.sum(jnp.where(piece_row == number, base, 0.0), axis=0, keepdims=True)
    label_place = order(target_row) * ROWS + CAP * SPAN + rank_row
    rows = select_ref.shape[0]
    select_ref[...] = one(iota((rows, tokens), 0) == place, jnp.bfloat16)
    label_at = one(iota((rows, pieces), 0) == label_place, jnp.bfloat16)
    labels = jnp.broadcast_to(slot_col + 1.0, (pieces, label_ref.shape[1])).astype(jnp.bfloat16)
    label_ref[...] = jnp.dot(label_at, labels, preferred_element_type=jnp.float32)


def prepare_tables(piece_row, target_row, slot_row, select, label_part, turn, spread_label):
    place_rows(piece_row, target_row, slot_row, select, label_part)
    out_row, lane = iota(turn.shape, 0), iota(turn.shape, 1)
    wanted = jnp.where(out_row < 32.0, 2.0 * out_row, jnp.where(out_row < 64.0, 2.0 * out_row - 63.0, 0.0))
    turn[...] = one(lane == wanted, jnp.bfloat16)
    source = lax.broadcasted_iota(jnp.int32, spread_label.shape, 0)
    goal = lax.broadcasted_iota(jnp.int32, spread_label.shape, 1)
    inside = goal & (ROWS - 1)
    label_row = goal - inside + CAP * SPAN + jnp.where(inside >= SPAN, 1, 0)
    spread_label[...] = one((source == label_row) & (inside < CAP * SPAN), jnp.bfloat16)


def gram_kernel(
    hidden_hbm, grads_hbm, in_hbm, out_hbm, piece_hbm, target_hbm, slot_hbm, result_ref,
    piece_ref, target_ref, slot_ref, hidden, grads, held, acc_in, acc_out, select, label_part, turn, spread_label, low, packed, owned_rows,
    feature, mixed, terms, gathered, load_sem, recv_sem, send_sem, edge_sem, inner_sem, swap_send, swap_recv, round_sem, left_recv,
):
    d, f = lax.axis_index("dp"), lax.axis_index("fsdp")
    p, y = d // NY, d % NY
    x, h, c = f // 4, (f // 2) % 2, f % 2
    wide_in, wide_out = in_hbm.shape[1], out_hbm.shape[1]
    step_rows = held.shape[1] // PARTS

    def name(x_, h_, c_):
        return x_ * 4 + h_ * 2 + c_

    def along_z(steps):
        z_ = (h * NZ + p + steps + 2 * NZ) % (2 * NZ)
        return ((z_ % NZ) * NY + y, name(x, z_ // NZ, c))

    def along_y(steps):
        return (p * NY + (y + steps + NY) % NY, f)

    east, west, far = (x + 1) % NX, (x + 3) % NX, (x + 2) % NX
    to_east, to_west, to_twin = (d, name(east, h, c)), (d, name(west, h, c)), (d, name(x, h, 1 - c))
    to_up, to_down = along_z(1), along_z(-1)
    to_far = (d, name(far, h, c))
    half = p // 3
    depth = p + half * (5 - 2 * p)
    to_inner = tuple((1 - half) * a + half * b for a, b in zip(to_up, to_down))
    to_outer = tuple((1 - half) * b + half * a for a, b in zip(to_up, to_down))

    def member(other):
        x_, c_ = (x + other // 4) % NX, (c + other % 2) % 2
        y_ = y + ((other // 2) % 2) * (1 - 2 * (y % 2))
        return (p * NY + y_, name(x_, h, c_)), name(x_, (y_ + p) % 2, c_)

    barrier = pltpu.get_barrier_semaphore()
    for peer in (to_east, to_west, to_far, to_twin, to_up, to_down, along_y(1), along_y(-1)):
        pl.semaphore_signal(barrier, inc=1, device_id=peer, device_id_type=MESH)

    loads = (
        pltpu.make_async_copy(in_hbm, held.at[f, :, pl.ds(0, wide_in)], load_sem.at[0]),
        pltpu.make_async_copy(out_hbm, held.at[f, :, pl.ds(wide_in, wide_out)], load_sem.at[1]),
        pltpu.make_async_copy(grads_hbm, grads, load_sem.at[2]),
        pltpu.make_async_copy(hidden_hbm, hidden, load_sem.at[3]),
        pltpu.make_async_copy(piece_hbm, piece_ref, load_sem.at[4]),
        pltpu.make_async_copy(target_hbm, target_ref, load_sem.at[5]),
        pltpu.make_async_copy(slot_hbm, slot_ref, load_sem.at[6]),
    )

    circles = (
        (to_east, to_west, to_twin), (to_twin,), (along_y(1), along_y(-1)), (along_y(2), along_y(-2)),
        (to_up, to_down), (along_z(2), along_z(-2)), (along_z(3), along_z(-3)),
    )

    def tell(number):
        for peer in circles[number]:
            pl.semaphore_signal(round_sem.at[number], inc=1, device_id=peer, device_id_type=MESH)

    def hear(number):
        pl.semaphore_wait(round_sem.at[number], len(circles[number]))

    def hear_and_tell(number):
        hear(number)
        tell(number + 1)

    def move(shard, part, peer, sem):
        piece = held.at[shard, pl.ds(pl.multiple_of(part * step_rows, step_rows), step_rows), :]
        return pltpu.make_async_remote_copy(
            src_ref=piece, dst_ref=piece, send_sem=sem, recv_sem=recv_sem.at[shard, part],
            device_id=peer, device_id_type=MESH,
        )

    def send(shard, part, *peers):
        for peer in peers:
            move(shard, part, peer, send_sem).start()

    def first_send(part, peer, sem):
        rows_ = pl.ds(part * step_rows, step_rows)
        for ref, lanes in ((in_hbm, pl.ds(0, wide_in)), (out_hbm, pl.ds(wide_in, wide_out))):
            pltpu.make_async_remote_copy(
                src_ref=ref.at[rows_, :], dst_ref=held.at[f, rows_, lanes], send_sem=sem, recv_sem=recv_sem.at[f, part],
                device_id=peer, device_id_type=MESH,
            ).start()

    def arrived(shard, part):
        move(shard, part, to_twin, send_sem).wait_recv()

    pl.semaphore_wait(barrier, 8)
    for q in range(PARTS):

        @pl.when(depth == 0)
        def _():
            first_send(q, to_outer, edge_sem)

        for peer in (to_east, to_west, to_far, to_twin):
            first_send(q, peer, send_sem)
    tell(0)
    for load in loads:
        load.start()

    def near(h_, q):
        part = q
        first, second = name(west, h_, c), name(east, h_, c)
        for shard in (first, second):
            arrived(shard, part)
            send(shard, part, to_twin)

    def remote(h_, q):
        shard, part = name(far, h_, c), q
        arrived(shard, part)
        send(shard, part, to_twin)

    across = name(x, 1 - h, c)

    for t in range(2 * PARTS):
        if t < 4:
            near(h, t)
        q = t - 2 * depth

        @pl.when(jnp.logical_and(q >= 0, q < PARTS))
        def _():
            part = q
            arrived(across, part)

            @pl.when(depth < 2)
            def _():
                move(across, part, to_inner, inner_sem).start()

            send(across, part, to_east, to_west, to_far, to_twin)

        if t < ROUNDS - 1:
            hear_and_tell(t)

    def use(shard):
        a = hidden[:, pl.ds(pl.multiple_of(shard * wide_in, 128), wide_in)]
        acc_in[...] += lax.dot_general(a, held[shard, :, :wide_in], nt, preferred_element_type=jnp.float32)
        b = grads[:, pl.ds(pl.multiple_of(shard * wide_out, 128), wide_out)]
        acc_out[...] += lax.dot_general(b, held[shard, :, wide_in:], nt, preferred_element_type=jnp.float32)

    def take(shard):
        for part in range(PARTS):
            arrived(shard, part)
        use(shard)

    nt = (((1,), (1,)), ((), ()))
    acc_in[...] = jnp.zeros_like(acc_in)
    acc_out[...] = jnp.zeros_like(acc_out)
    for load in loads[4:]:
        load.wait()
    prepare_tables(
        piece_ref[...].astype(jnp.float32), target_ref[...].astype(jnp.float32), slot_ref[...].astype(jnp.float32),
        select, label_part, turn, spread_label,
    )
    for load in loads[:4]:
        load.wait()
    remote(h, 0)
    remote(h, 1)
    remote(h, 2)
    remote(h, 3)
    near(1 - h, 0)
    near(1 - h, 1)
    near(1 - h, 2)
    near(1 - h, 3)
    for x_ in (x, west, east, far):
        use(name(x_, h, c))
    for x_ in (x, west, east, far):
        take(name(x_, h, 1 - c))
    for x_ in (x, west, east):
        use(name(x_, 1 - h, c))
    remote(1 - h, 0)
    remote(1 - h, 1)
    remote(1 - h, 2)
    remote(1 - h, 3)
    for x_ in (x, west, east):
        take(name(x_, 1 - h, 1 - c))
    use(name(far, 1 - h, c))
    take(name(far, 1 - h, 1 - c))
    hear(6)

    def drain(ref, count, sem):
        whole = ref.at[pl.ds(0, count)]
        pltpu.make_async_copy(whole, whole, sem).wait()

    low[:, :64] = acc_in[...].astype(low.dtype)
    low[:, 64:] = acc_out[...].astype(low.dtype)
    blocks = jnp.dot(select[...], low[...], preferred_element_type=jnp.float32) + label_part[...]
    packed[...] = blocks.astype(jnp.bfloat16).reshape(packed.shape)

    def post(src, dst, peer, phase):
        pltpu.make_async_remote_copy(
            src_ref=src, dst_ref=dst, send_sem=swap_send.at[phase], recv_sem=swap_recv.at[phase],
            device_id=peer, device_id_type=MESH,
        ).start()

    def keep(src, dst, phase):
        pltpu.make_async_copy(src, dst, swap_recv.at[phase]).start()

    keep(packed.at[SHIFT], owned_rows.at[SHIFT], 0)

    for k in sorted(range(EACH), key=lambda k: -abs(k - SHIFT))[:-1]:
        post(packed.at[k], owned_rows.at[k], ((d + k + ND - SHIFT) % ND, f), 0)

    drain(owned_rows, EACH, swap_recv.at[0])

    rows = owned_rows[...].reshape(EACH * ROWS, 128)
    turned = lax.dot_general(turn[...], rows, nt, preferred_element_type=jnp.float32)
    label_rows = jnp.dot(turned[64:80].astype(jnp.bfloat16), spread_label[...], preferred_element_type=jnp.float32)
    hit = one(label_rows[:1] == iota((OWN, EACH * ROWS), 0) + 1.0)
    high = iota(rows.shape, 1) >= 64.0
    rows32 = rows.astype(jnp.float32)
    value_odd = jnp.where(high, rows32, 0.0).astype(jnp.bfloat16)
    value_even = jnp.where(high, 0.0, pltpu.roll(rows32, 64, 1)).astype(jnp.bfloat16)

    def expand(block):
        wide = block[:, None, :] * hit[None]
        return wide.reshape(32 * OWN, EACH * ROWS).astype(jnp.bfloat16)

    made = jnp.dot(expand(turned[:32]), value_even, preferred_element_type=jnp.float32)
    made += jnp.dot(expand(turned[32:64]), value_odd, preferred_element_type=jnp.float32)
    feature[...] = made.astype(jnp.bfloat16).reshape(feature.shape)

    here = name(x, (y + p) % 2, c)
    keep(feature.at[here], mixed.at[2 * here], 1)
    keep(feature.at[0], mixed.at[2 * here + 1], 1)
    post(feature.at[0], mixed.at[2 * here + 1], to_twin, 1)
    same_core = range(GROUP - 2, 0, -2)
    for other in same_core:
        back = (NX - other // 4) % NX * 2 + (other // 2) % 2
        pltpu.make_async_remote_copy(
            src_ref=feature.at[0], dst_ref=mixed.at[2 * here + 1], send_sem=swap_send.at[1], recv_sem=left_recv.at[back],
            device_id=member(other)[0], device_id_type=MESH,
        ).start()
    for other in range(GROUP - 1, 0, -1):
        peer, columns = member(other)
        post(feature.at[columns], mixed.at[2 * here], peer, 1)
    for other in sorted(same_core, key=lambda o: (o // 4) % 2 + 2 * (o // 8 % 2) * (1 - (o // 4) % 2) + (o // 2) % 2):
        block = mixed.at[2 * member(other)[1] + 1]
        pltpu.make_async_copy(block, block, left_recv.at[other // 2]).wait()
        post(block, block, to_twin, 1)
    drain(mixed, 2 * GROUP - 7, swap_recv.at[1])

    both = mixed[...].astype(jnp.float32).reshape(GROUP, 2, 2, OWN, 128)
    tn = (((0,), (0,)), ((), ()))

    def side(which, pair):
        return both[:, which, pair].reshape(GROUP * OWN, 128).astype(jnp.bfloat16)

    lefts = (side(1, 0), side(1, 1))
    tiles = []
    for pair in range(2):
        right = side(0, pair)
        top = lax.dot_general(lefts[0], right, tn, preferred_element_type=jnp.float32)
        low_part = lax.dot_general(lefts[1], right, tn, preferred_element_type=jnp.float32)
        tiles.append(jnp.concatenate([top, low_part[: GR - 128]], axis=0).reshape(GR // 8, 8, 128))
    upper = lax.broadcasted_iota(jnp.int32, tiles[0].shape, 1) < 4
    terms[:, 0] = jnp.where(upper, tiles[0], pltpu.roll(tiles[1], 4, 1)).astype(terms.dtype)
    terms[:, 1] = jnp.where(upper, pltpu.roll(tiles[0], 4, 1), tiles[1]).astype(terms.dtype)

    column = name(x, (y + p) % 2, c)
    mine = h * (ND // 2) + p * (NY // 2) + y // 2
    at_home = ((y + p) % 2) == h

    def term(o):
        return terms.at[o // 2, o % 2]

    start = d + jnp.where(at_home, ND // 2, 0)

    @pl.loop(0, ND)
    def _(j):
        o = (start + j) % ND
        here_too = jnp.logical_and(at_home, o == d)

        @pl.when(here_too)
        def _():
            keep(term(o), gathered.at[mine], 2)

        @pl.when(jnp.logical_not(here_too))
        def _():
            post(term(o), gathered.at[mine], (o, column), 2)

    drain(gathered, ND, swap_recv.at[2])
    total = jnp.sum(gathered[...].astype(jnp.float32), axis=0)
    result_ref[:, :128] = total[:4]
    result_ref[:, 128:] = total[4:]

    drain(held, 14, send_sem)

    @pl.when(depth == 0)
    def _():
        drain(held, 1, edge_sem)

    @pl.when(depth < 2)
    def _():
        drain(held, 1, inner_sem)

    drain(packed, EACH - 1, swap_send.at[0])
    drain(mixed, 2 * (GROUP - 1), swap_send.at[1])

    @pl.when(at_home)
    def _():
        drain(gathered, ND - 1, swap_send.at[2])

    @pl.when(jnp.logical_not(at_home))
    def _():
        drain(gathered, ND, swap_send.at[2])


def on_device(hidden_in, out_grads, piece_of, owner_dp, owner_slot, sketch_in, sketch_out):
    rows = hidden_in.shape[0]
    width = sketch_in.shape[1]
    wide = sketch_in.shape[0] + sketch_out.shape[0]
    anywhere = pl.BlockSpec(memory_space=pl.ANY)
    vmem = pl.BlockSpec(memory_space=pltpu.VMEM)
    bf16, f32 = jnp.bfloat16, jnp.float32
    total = pl.pallas_call(
        gram_kernel,
        out_shape=jax.ShapeDtypeStruct((GR // ND, 4096 // GROUP), f32),
        in_specs=[anywhere] * 7,
        out_specs=vmem,
        scratch_shapes=[
            pltpu.VMEM(piece_of.shape, jnp.int32),
            pltpu.VMEM(owner_dp.shape, jnp.int32),
            pltpu.VMEM(owner_slot.shape, jnp.int32),
            pltpu.VMEM(hidden_in.shape, bf16),
            pltpu.VMEM(out_grads.shape, bf16),
            pltpu.VMEM((GROUP, width, wide), bf16),
            pltpu.VMEM((rows, width), f32),
            pltpu.VMEM((rows, width), f32),
            pltpu.VMEM((EACH * ROWS, rows), bf16),
            pltpu.VMEM((EACH * ROWS, 128), f32),
            pltpu.VMEM((80, 128), bf16),
            pltpu.VMEM((EACH * ROWS, EACH * ROWS), bf16),
            pltpu.VMEM((rows, 128), bf16),
            pltpu.VMEM((EACH, ROWS, 128), bf16),
            pltpu.VMEM((EACH, ROWS, 128), bf16),
            pltpu.VMEM((GROUP, 2 * OWN, 128), bf16),
            pltpu.VMEM((2 * GROUP, 2 * OWN, 128), bf16),
            pltpu.VMEM((GR // 8, 2, 8, 128), bf16),
            pltpu.VMEM((ND, 8, 128), bf16),
            pltpu.SemaphoreType.DMA((7,)),
            pltpu.SemaphoreType.DMA((GROUP, PARTS)),
            pltpu.SemaphoreType.DMA,
            pltpu.SemaphoreType.DMA,
            pltpu.SemaphoreType.DMA,
            pltpu.SemaphoreType.DMA((3,)),
            pltpu.SemaphoreType.DMA((3,)),
            pltpu.SemaphoreType.REGULAR((ROUNDS,)),
            pltpu.SemaphoreType.DMA((GROUP // 2,)),
        ],
        compiler_params=pltpu.CompilerParams(collective_id=0, has_side_effects=True),
        name="gram",
    )(hidden_in, out_grads, sketch_in.T, sketch_out.T, piece_of, owner_dp, owner_slot)
    return total * (1.0 / math.sqrt(OWN * ND * GROUP))


def solution(mesh):
    return jax.shard_map(
        on_device,
        mesh=mesh,
        in_specs=(
            P(("dp", "fsdp"), None),
            P(("dp", "fsdp"), None),
            P(("dp", "fsdp"), None),
            P(("dp", "fsdp"), None),
            P(("dp", "fsdp"), None),
            P("fsdp", None),
            P("fsdp", None),
        ),
        out_specs=P("dp", "fsdp"),
        check_vma=False,
    )
```
